32 devices in a mesh: img: 4 (over x, core), tok: 8 (over z, y).
Axes of the slice: x: 2, y: 2, z: 4, core: 2. Of those that a mesh axis runs over, the one named last changes fastest.
Arguments:
- student: bfloat16 [4, 1024, 4096], P('img', None, 'tok'), may hold values from -0.32 to 0.32
- teacher: bfloat16 [4, 64, 64, 4096], P('img', None, None, 'tok'), may hold values from -160 to 160
Outputs:
- gradient: bfloat16 [4, 1024, 4096], P('img', None, 'tok')
- loss: float32 [], replicated
The draws below stay inside these ranges and needn't reach their ends.
All inputs are finite; a program needn't handle non-finite values.
Results may differ from the reference program's by a relative error of at most 0.0069.
Values may be sent and summed in bfloat16 or wider, within the bound.
A program may use at most 64 MiB of HBM per device.

```python
import math
import jax
import jax.numpy as jnp
from jax import lax

D = 4096
GH = 32
GW = 32
HRH = 64
HRW = 64
P_SIZE = 1024
IMAGES = 4


def feature_values(key, shape, width, base_scale):
    first = jax.random.fold_in(key, 0)
    position = jnp.arange(width, dtype=jnp.float32) / max(width - 1, 1)
    ramp = jnp.exp(position * math.log(3.0))
    noise = jnp.clip(jax.random.normal(first, shape, jnp.float32), -4.0, 4.0)
    return base_scale * noise * ramp


def draw_student(key, part):
    values = feature_values(jax.random.fold_in(key, 11), (IMAGES, P_SIZE, D), D, 0.002)
    return values.astype(jnp.bfloat16)


def draw_teacher(key, part):
    values = feature_values(jax.random.fold_in(key, 23), (IMAGES, HRH, HRW, D), D, 1.0)
    return values.astype(jnp.bfloat16)


def setup_inputs(seed: int = 0) -> dict:
    keys = jax.random.split(jax.random.key(seed), 3)
    return {
        "student": draw_student(jax.random.fold_in(keys[2], 71), 0),
        "teacher": draw_teacher(jax.random.fold_in(keys[2], 71), 0),
    }


cubic_taps = (-0.09375, 0.59375, 0.59375, -0.09375)
epsilon = 1e-06

def shrink(padded, length, dimension):
    weighted = [cubic_taps[offset] * lax.slice_in_dim(padded, offset, offset + 2 * length - 1, 2, dimension).astype(jnp.float32) for offset in range(4)]
    return weighted[0] + weighted[1] + weighted[2] + weighted[3]

def one_image(inputs):
    student_rows, teacher_grid = inputs
    padded = jnp.pad(teacher_grid, ((1, 1), (1, 1), (0, 0)), mode='edge')
    vertical = shrink(padded, GH, 0)
    shrunk = shrink(vertical, GW, 1).reshape(P_SIZE, D)
    teacher_unit = (shrunk * lax.rsqrt(lax.optimization_barrier(jnp.sum(shrunk * shrunk, axis=1, keepdims=True)) + epsilon)).astype(jnp.bfloat16)
    features = student_rows.astype(jnp.float32)
    inverse = lax.rsqrt(lax.optimization_barrier(jnp.sum(features * features, axis=1, keepdims=True)) + epsilon)
    unit_rows = features * inverse
    unit_low = unit_rows.astype(jnp.bfloat16)
    mismatch = jnp.dot(unit_low, unit_low.T, preferred_element_type=jnp.float32) - jnp.dot(teacher_unit, teacher_unit.T, preferred_element_type=jnp.float32)
    squared = jnp.sum(mismatch * mismatch)
    pull_grad = 4.0 * jnp.dot(mismatch.astype(jnp.bfloat16), unit_low, preferred_element_type=jnp.float32)
    gradient = inverse * pull_grad - inverse * unit_rows * lax.optimization_barrier(jnp.sum(unit_rows * pull_grad, axis=1, keepdims=True))
    return (gradient.astype(jnp.bfloat16), squared)

def reference(student, teacher):
    gradients, losses = lax.map(one_image, (student, teacher))
    return (gradients, jnp.sum(losses) / P_SIZE)
```

```python
import functools

import jax
import jax.numpy as jnp
from jax import lax
from jax.experimental import pallas as pl
from jax.experimental.pallas import tpu as pltpu
from jax.sharding import PartitionSpec as P

cubic_taps = (-0.09375, 0.59375, 0.59375, -0.09375)
epsilon = 1e-06
LANES = 128
BLOCK = 256
LAG = 1


def lane_tiles_sum(x):
    total = x[:, :LANES]
    for start in range(LANES, x.shape[1], LANES):
        total = total + x[:, start : start + LANES]
    return total


def spread(column, width):
    return jnp.concatenate([column] * (width // LANES), axis=1)


def kernel(
    sizes, student_hbm, teacher_hbm, taps_ref, out_ref, loss_ref,
    sbuf, tbuf, hbuf, shrunk, unit_low, teach_low, part, inv, tinv,
    snorm, tnorm, along, losses, img_losses,
    own, ysend, yrecv, zin, zout, mlow, pull, sqacc,
    load_sem, s_send, s_recv, t_send, t_recv, a_send, a_recv, l_send, l_recv,
    i_send, i_recv, y_send, y_recv, z_send, z_recv, g_send, g_recv,
):
    n, m = sizes
    tokens, feats = unit_low.shape
    height, width = tbuf.shape[0], tbuf.shape[1]
    group = load_sem.shape[0] - 1
    rows_per = height // group
    half_w = width // 2
    nb = tokens // BLOCK
    tiles = tokens // LANES
    me = lax.axis_index("tok")
    img = lax.axis_index("img")
    col = lax.rem(me, 2)
    row = me // 2
    chain = n // 2
    pairs = [(i, j) for i in range(nb) for j in range(i, nb)]
    count = len(pairs) // 2
    early = jnp.where(row < (chain + 1) // 2, 0, 1)
    late = 1 - early
    rank = jnp.minimum(row, chain - 1 - row)

    def load(g):
        rows = pl.ds(g * rows_per, rows_per)
        return pltpu.make_async_copy(
            teacher_hbm.at[0, rows], tbuf.at[rows], load_sem.at[g]
        )

    student_load = pltpu.make_async_copy(student_hbm.at[0], sbuf, load_sem.at[group])
    student_load.start()

    @pl.loop(0, group)
    def _(g):
        load(g).start()

    barrier = pltpu.get_barrier_semaphore()
    for p in range(1, n):
        pl.semaphore_signal(barrier, 1, device_id={"tok": lax.rem(me + p, n)})
    for p in range(1, m):
        pl.semaphore_signal(barrier, 1, device_id={"img": lax.rem(img + p, m)})

    def gather_copies(buf, send, recv, axis, here, size):
        return [
            pltpu.make_async_remote_copy(
                src_ref=buf.at[here],
                dst_ref=buf.at[here],
                send_sem=send.at[p - 1],
                recv_sem=recv.at[p - 1],
                device_id={axis: lax.rem(here + p, size)},
            )
            for p in range(1, size)
        ]

    def pack_rows(buf):
        @pl.loop(0, tiles)
        def _(b):
            block = part[pl.ds(pl.multiple_of(b * LANES, LANES), LANES), :]
            buf[me, pl.ds(b, 1), :] = jnp.sum(block.T, axis=0, keepdims=True)

    def summed(buf, size):
        total = buf[0]
        for k in range(1, size):
            total = total + buf[k]
        return total

    def unpack_rows(values, dst):
        for b in range(tiles):
            dst[b * LANES : (b + 1) * LANES, :] = jnp.broadcast_to(
                values[b : b + 1, :], (LANES, LANES)
            ).T

    def slab(b):
        return pl.ds(pl.multiple_of(b * LANES, LANES), LANES)

    @pl.when(rank == 0)
    def _():
        zin[early] = jnp.zeros(zin.shape[1:], zin.dtype)

    sqacc[...] = jnp.zeros_like(sqacc)
    student_load.wait()

    @pl.loop(0, tiles)
    def _(b):
        x = sbuf[slab(b), :].astype(jnp.float32)
        part[slab(b), :] = lane_tiles_sum(x * x)

    pack_rows(snorm)
    pl.semaphore_wait(barrier, n - 1 + m - 1)
    s_copies = gather_copies(snorm, s_send, s_recv, "tok", me, n)
    for copy in s_copies:
        copy.start()

    @pl.loop(0, group)
    def _(g):
        load(g).wait()
        x = tbuf[pl.ds(g * rows_per, rows_per)].reshape(rows_per * width, feats)
        y = jnp.dot(taps_ref[...], x, preferred_element_type=jnp.float32)
        hbuf[pl.ds(g * rows_per + 1, rows_per)] = y.reshape(rows_per, half_w, feats)

    hbuf[0] = hbuf[1]
    hbuf[height + 1] = hbuf[height]

    @pl.loop(0, height // 2)
    def _(a):
        v = cubic_taps[0] * hbuf[2 * a]
        for k in range(1, 4):
            v = v + cubic_taps[k] * hbuf[2 * a + k]
        rows = pl.ds(pl.multiple_of(a * half_w, half_w), half_w)
        shrunk[rows, :] = v
        part[rows, :] = lane_tiles_sum(v * v)

    pack_rows(tnorm)
    t_copies = gather_copies(tnorm, t_send, t_recv, "tok", me, n)
    for copy in t_copies:
        copy.start()

    for copy in s_copies:
        copy.wait_recv()
    unpack_rows(lax.rsqrt(summed(snorm, n) + epsilon), inv)

    @pl.loop(0, tiles)
    def _(b):
        x = sbuf[slab(b), :].astype(jnp.float32) * spread(inv[slab(b), :], feats)
        unit_low[slab(b), :] = x.astype(jnp.bfloat16)

    def pick(k, c):
        first, second = pairs[k], pairs[count + k]
        i = first[0] + c * (second[0] - first[0])
        j = first[1] + c * (second[1] - first[1])
        return i, j

    def strip(i):
        return pl.ds(pl.multiple_of(i * BLOCK, BLOCK), BLOCK)

    def gram(low, i, j):
        return lax.dot_general(
            low[strip(i), :], low[strip(j), :], (((1,), (1,)), ((), ())),
            preferred_element_type=jnp.float32,
        )

    for k in range(count):
        own[count + k] = gram(unit_low, *pick(k, 1 - col))
    for k in range(count):
        own[k] = gram(unit_low, *pick(k, col))

    for copy in t_copies:
        copy.wait_recv()
    unpack_rows(lax.rsqrt(summed(tnorm, n) + epsilon), tinv)

    @pl.loop(0, tiles)
    def _(b):
        x = shrunk[slab(b), :] * spread(tinv[slab(b), :], feats)
        teach_low[slab(b), :] = x.astype(jnp.bfloat16)

    y_copies = []
    for k in range(count):
        d = own[count + k] - gram(teach_low, *pick(k, 1 - col))
        ysend[k] = d.astype(jnp.bfloat16)
        copy = pltpu.make_async_remote_copy(
            src_ref=ysend.at[k], dst_ref=yrecv.at[k],
            send_sem=y_send.at[k], recv_sem=y_recv.at[k],
            device_id={"tok": me + 1 - 2 * col},
        )
        copy.start()
        y_copies.append(copy)
    for k in range(count):
        own[k] = own[k] - gram(teach_low, *pick(k, col))

    def chain_copy(direction, k):
        step = 2 - 4 * direction
        return pltpu.make_async_remote_copy(
            src_ref=zout.at[direction, k], dst_ref=zin.at[direction, k],
            send_sem=z_send.at[direction, k], recv_sem=z_recv.at[direction, k],
            device_id={"tok": lax.rem(me + step + n, n)},
        )

    def block_copy(k):
        i, j = pick(k, col)
        block = mlow.at[strip(i), strip(j)]
        return pltpu.make_async_remote_copy(
            src_ref=block, dst_ref=block,
            send_sem=g_send.at[k], recv_sem=g_recv.at[k],
            device_id={"tok": me + 1 - 2 * col},
        )

    def run_early(k):
        y_copies[k].wait_recv()
        mine = own[k] + yrecv[k].astype(jnp.float32)
        copy = chain_copy(early, k)

        @pl.when(rank > 0)
        def _():
            copy.wait_recv()

        total = mine + zin[early, k].astype(jnp.float32)
        zout[early, k] = total.astype(jnp.bfloat16)
        own[k] = mine
        own[count + k] = total
        copy.start()

    def run_late(k):
        copy = chain_copy(late, k)
        copy.wait_recv()
        incoming = zin[late, k].astype(jnp.float32)
        total = own[count + k] + incoming
        i, j = pick(k, col)
        low = total.astype(jnp.bfloat16)

        @pl.when(rank > 0)
        def _():
            zout[late, k] = (own[k] + incoming).astype(jnp.bfloat16)
            copy.start()

        mlow[strip(i), strip(j)] = low
        block_copy(k).start()
        weight = jnp.where(i == j, 1.0, 2.0)
        sqacc[...] += weight * jnp.sum(total * total, axis=0, keepdims=True)

        @pl.when(i != j)
        def _():
            mlow[strip(j), strip(i)] = total.T.astype(jnp.bfloat16)

    for t in range(count + LAG):
        if t < count:
            run_early(t)
        if t >= LAG:
            run_late(t - LAG)

    squared = jnp.sum(sqacc[...], axis=1, keepdims=True)
    losses[me] = jnp.broadcast_to(squared, losses.shape[1:])
    l_copies = gather_copies(losses, l_send, l_recv, "tok", me, n)
    for copy in l_copies:
        copy.start()

    for k in range(count):
        block_copy(k).wait_recv()
        i, j = pick(k, 1 - col)

        @pl.when(i != j)
        def _():
            block = mlow[strip(i), strip(j)].astype(jnp.float32)
            mlow[strip(j), strip(i)] = block.T.astype(jnp.bfloat16)

    @pl.loop(0, nb)
    def _(b):
        rows = strip(b)
        p = 4.0 * jnp.dot(mlow[rows, :], unit_low[...], preferred_element_type=jnp.float32)
        pull[rows, :] = p
        unit = sbuf[rows, :].astype(jnp.float32) * spread(inv[rows, :], feats)
        part[rows, :] = lane_tiles_sum(unit * p)

    pack_rows(along)
    a_copies = gather_copies(along, a_send, a_recv, "tok", me, n)
    for copy in a_copies:
        copy.start()

    for copy in l_copies:
        copy.wait_recv()
    img_losses[img] = summed(losses, n)
    i_copies = gather_copies(img_losses, i_send, i_recv, "img", img, m)
    for copy in i_copies:
        copy.start()

    for copy in a_copies:
        copy.wait_recv()
    unpack_rows(summed(along, n), tinv)

    @pl.loop(0, tiles)
    def _(b):
        scale = spread(inv[slab(b), :], feats)
        unit = sbuf[slab(b), :].astype(jnp.float32) * scale
        grad = scale * pull[slab(b), :] - scale * unit * spread(tinv[slab(b), :], feats)
        out_ref[0, slab(b), :] = grad.astype(out_ref.dtype)

    for copy in i_copies:
        copy.wait_recv()
    loss_ref[...] = summed(img_losses, m) / (chain * tokens)

    for copy in s_copies + t_copies + l_copies + a_copies + i_copies + y_copies:
        copy.wait_send()
    for k in range(count):
        block_copy(k).wait_send()
        chain_copy(early, k).wait_send()

        @pl.when(rank > 0)
        def _():
            chain_copy(late, k).wait_send()


def tap_matrix(width, rows_per):
    half = width // 2
    source = jnp.arange(width)[None, :]
    taps = jnp.zeros((half, width), jnp.float32)
    for q in range(4):
        wanted = jnp.clip(2 * jnp.arange(half)[:, None] - 1 + q, 0, width - 1)
        taps = taps + jnp.where(source == wanted, cubic_taps[q], 0.0)
    return jnp.kron(jnp.eye(rows_per, dtype=jnp.float32), taps).astype(jnp.bfloat16)


def per_device(n, m, student, teacher):
    _, tokens, feats = student.shape
    _, height, width, _ = teacher.shape
    rows_per = max(1, 256 // width)
    groups = height // rows_per
    nb = tokens // BLOCK
    count = nb * (nb + 1) // 4
    tiles = tokens // LANES
    f32, bf16 = jnp.float32, jnp.bfloat16
    vmem, dma = pltpu.VMEM, pltpu.SemaphoreType.DMA
    gradient, loss = pl.pallas_call(
        functools.partial(kernel, (n, m)),
        name="anchor",
        out_shape=(
            jax.ShapeDtypeStruct(student.shape, bf16),
            jax.ShapeDtypeStruct((8, LANES), f32),
        ),
        in_specs=[
            pl.BlockSpec(memory_space=pl.ANY),
            pl.BlockSpec(memory_space=pl.ANY),
            pl.BlockSpec(memory_space=pltpu.VMEM),
        ],
        out_specs=(
            pl.BlockSpec(memory_space=pltpu.VMEM),
            pl.BlockSpec(memory_space=pltpu.VMEM),
        ),
        scratch_shapes=[
            vmem((tokens, feats), bf16),
            vmem((height, width, feats), bf16),
            vmem((height + 2, width // 2, feats), f32),
            vmem((tokens, feats), f32),
            vmem((tokens, feats), bf16),
            vmem((tokens, feats), bf16),
            vmem((tokens, LANES), f32),
            vmem((tokens, LANES), f32),
            vmem((tokens, LANES), f32),
            vmem((n, tiles, LANES), f32),
            vmem((n, tiles, LANES), f32),
            vmem((n, tiles, LANES), f32),
            vmem((n, 8, LANES), f32),
            vmem((m, 8, LANES), f32),
            vmem((2 * count, BLOCK, BLOCK), f32),
            vmem((count, BLOCK, BLOCK), bf16),
            vmem((count, BLOCK, BLOCK), bf16),
            vmem((2, count, BLOCK, BLOCK), bf16),
            vmem((2, count, BLOCK, BLOCK), bf16),
            vmem((tokens, tokens), bf16),
            vmem((tokens, feats), f32),
            vmem((1, BLOCK), f32),
            dma((groups + 1,)),
            dma((n - 1,)), dma((n - 1,)), dma((n - 1,)), dma((n - 1,)),
            dma((n - 1,)), dma((n - 1,)), dma((n - 1,)), dma((n - 1,)),
            dma((m - 1,)), dma((m - 1,)),
            dma((count,)), dma((count,)),
            dma((2, count)), dma((2, count)),
            dma((count,)), dma((count,)),
        ],
        compiler_params=pltpu.CompilerParams(
            collective_id=0, has_side_effects=True, vmem_limit_bytes=56 * 1024 * 1024
        ),
    )(student, teacher, tap_matrix(width, rows_per))
    return gradient, loss[0, 0]


def solution(mesh):
    return jax.shard_map(
        functools.partial(per_device, mesh.shape["tok"], mesh.shape["img"]),
        mesh=mesh,
        in_specs=(P("img", None, "tok"), P("img", None, None, "tok")),
        out_specs=(P("img", None, "tok"), P()),
        check_vma=False,
    )
```

```python
import functools

import jax
import jax.numpy as jnp
import numpy as np
from jax import lax
from jax.experimental import pallas as pl
from jax.experimental.pallas import tpu as pltpu
from jax.sharding import PartitionSpec as P

cubic_taps = (-0.09375, 0.59375, 0.59375, -0.09375)
epsilon = 1e-06
LANES = 128
BLOCK = 256
SPLIT = 2
LAG = 2


def lane_tiles_sum(x):
    total = x[:, :LANES]
    for start in range(LANES, x.shape[1], LANES):
        total = total + x[:, start : start + LANES]
    return total


def spread(column, width):
    return jnp.concatenate([column] * (width // LANES), axis=1)


def kernel(
    sizes, student_hbm, teacher_hbm, taps_ref, out_ref, loss_ref,
    sbuf, tbuf, hbuf, shrunk, unit_low, teach_low, part, inv, tinv,
    snorm, tnorm, along, losses, img_losses,
    own, prefix, theirs, ysend, yrecv, zin, zout, mlow, pull, sqacc,
    load_sem, s_send, s_recv, t_send, t_recv, a_send, a_recv, l_send, l_recv,
    i_send, i_recv, y_send, y_recv, z_send, z_recv, g_send, g_recv,
):
    n, m = sizes
    tokens, feats = unit_low.shape
    height, width = tbuf.shape[0], tbuf.shape[1]
    group = load_sem.shape[0] - 1
    rows_per = height // group
    half_w = width // 2
    nb = tokens // BLOCK
    tiles = tokens // LANES
    me = lax.axis_index("tok")
    img = lax.axis_index("img")
    col = lax.rem(me, 2)
    row = me // 2
    chain = n // 2
    pairs = [(i, j) for i in range(nb) for j in range(i, nb)]
    half = len(pairs) // 2
    count = half * SPLIT
    depth = BLOCK // SPLIT
    early = jnp.where(row < (chain + 1) // 2, 0, 1)
    late = 1 - early
    rank = jnp.minimum(row, chain - 1 - row)

    def load(g):
        rows = pl.ds(g * rows_per, rows_per)
        return pltpu.make_async_copy(
            teacher_hbm.at[0, rows], tbuf.at[rows], load_sem.at[g]
        )

    student_load = pltpu.make_async_copy(student_hbm.at[0], sbuf, load_sem.at[group])
    student_load.start()

    @pl.loop(0, group)
    def _(g):
        load(g).start()

    barrier = pltpu.get_barrier_semaphore()
    for p in range(1, n):
        pl.semaphore_signal(barrier, 1, device_id={"tok": lax.rem(me + p, n)})
    for p in range(1, m):
        pl.semaphore_signal(barrier, 1, device_id={"img": lax.rem(img + p, m)})

    def gather_copies(buf, send, recv, axis, here, size):
        return [
            pltpu.make_async_remote_copy(
                src_ref=buf.at[here],
                dst_ref=buf.at[here],
                send_sem=send.at[p - 1],
                recv_sem=recv.at[p - 1],
                device_id={axis: lax.rem(here + p, size)},
            )
            for p in range(1, size)
        ]

    def pack_rows(buf):
        @pl.loop(0, tiles)
        def _(b):
            block = part[pl.ds(pl.multiple_of(b * LANES, LANES), LANES), :]
            buf[me, pl.ds(b, 1), :] = jnp.sum(block.T, axis=0, keepdims=True)

    def summed(buf, size):
        total = buf[0]
        for k in range(1, size):
            total = total + buf[k]
        return total

    def unpack_rows(values, dst):
        for b in range(tiles):
            dst[b * LANES : (b + 1) * LANES, :] = jnp.broadcast_to(
                values[b : b + 1, :], (LANES, LANES)
            ).T

    def slab(b):
        return pl.ds(pl.multiple_of(b * LANES, LANES), LANES)

    @pl.when(rank == 0)
    def _():
        zin[early] = jnp.zeros(zin.shape[1:], zin.dtype)

    sqacc[...] = jnp.zeros_like(sqacc)
    student_load.wait()

    @pl.loop(0, tiles)
    def _(b):
        x = sbuf[slab(b), :].astype(jnp.float32)
        part[slab(b), :] = lane_tiles_sum(x * x)

    pack_rows(snorm)
    @pl.loop(0, group)
    def _(g):
        load(g).wait()
        x = tbuf[pl.ds(g * rows_per, rows_per)].reshape(rows_per * width, feats)
        y = jnp.dot(taps_ref[...], x, preferred_element_type=jnp.float32)
        hbuf[pl.ds(g * rows_per + 1, rows_per)] = y.reshape(rows_per, half_w, feats)

    pl.semaphore_wait(barrier, n - 1 + m - 1)
    s_copies = gather_copies(snorm, s_send, s_recv, "tok", me, n)
    for copy in s_copies:
        copy.start()

    hbuf[0] = hbuf[1]
    hbuf[height + 1] = hbuf[height]

    @pl.loop(0, height // 2)
    def _(a):
        v = cubic_taps[0] * hbuf[2 * a]
        for k in range(1, 4):
            v = v + cubic_taps[k] * hbuf[2 * a + k]
        rows = pl.ds(pl.multiple_of(a * half_w, half_w), half_w)
        shrunk[rows, :] = v
        part[rows, :] = lane_tiles_sum(v * v)

    pack_rows(tnorm)
    t_copies = gather_copies(tnorm, t_send, t_recv, "tok", me, n)
    for copy in t_copies:
        copy.start()

    for copy in s_copies:
        copy.wait_recv()
    unpack_rows(lax.rsqrt(summed(snorm, n) + epsilon), inv)

    @pl.loop(0, tiles)
    def _(b):
        x = sbuf[slab(b), :].astype(jnp.float32) * spread(inv[slab(b), :], feats)
        unit_low[slab(b), :] = x.astype(jnp.bfloat16)

    def pick(k, c):
        first, second = pairs[k], pairs[half + k]
        i = first[0] + c * (second[0] - first[0])
        j = first[1] + c * (second[1] - first[1])
        return i, j

    def strip(i):
        return pl.ds(pl.multiple_of(i * BLOCK, BLOCK), BLOCK)

    def gram(low, i, j):
        return lax.dot_general(
            low[strip(i), :], low[strip(j), :], (((1,), (1,)), ((), ())),
            preferred_element_type=jnp.float32,
        )

    for k in range(half):
        theirs[k] = gram(unit_low, *pick(k, 1 - col))
    for k in range(half):
        pieces = gram(unit_low, *pick(k, col))
        own[k * SPLIT : (k + 1) * SPLIT] = pieces.reshape(SPLIT, depth, BLOCK)

    for copy in t_copies:
        copy.wait_recv()
    unpack_rows(lax.rsqrt(summed(tnorm, n) + epsilon), tinv)

    @pl.loop(0, tiles)
    def _(b):
        x = shrunk[slab(b), :] * spread(tinv[slab(b), :], feats)
        teach_low[slab(b), :] = x.astype(jnp.bfloat16)

    y_copies = []
    for k in range(half):
        d = theirs[k] - gram(teach_low, *pick(k, 1 - col))
        pieces = d.astype(jnp.bfloat16).reshape(SPLIT, depth, BLOCK)
        ysend[k * SPLIT : (k + 1) * SPLIT] = pieces
        for t in range(k * SPLIT, (k + 1) * SPLIT):
            copy = pltpu.make_async_remote_copy(
                src_ref=ysend.at[t], dst_ref=yrecv.at[t],
                send_sem=y_send.at[t], recv_sem=y_recv.at[t],
                device_id={"tok": me + 1 - 2 * col},
            )
            copy.start()
            y_copies.append(copy)
    for k in range(half):
        d = gram(teach_low, *pick(k, col)).reshape(SPLIT, depth, BLOCK)
        own[k * SPLIT : (k + 1) * SPLIT] = own[k * SPLIT : (k + 1) * SPLIT] - d

    def chain_copy(direction, k):
        step = 2 - 4 * direction
        return pltpu.make_async_remote_copy(
            src_ref=zout.at[direction, k], dst_ref=zin.at[direction, k],
            send_sem=z_send.at[direction, k], recv_sem=z_recv.at[direction, k],
            device_id={"tok": lax.rem(me + step + n, n)},
        )

    def piece(k, c):
        i, j = pick(k // SPLIT, c)
        start = i * BLOCK + (k % SPLIT) * depth
        return i, j, pl.ds(pl.multiple_of(start, depth), depth)

    def block_copy(k):
        i, j, rows = piece(k, col)
        block = mlow.at[rows, strip(j)]
        return pltpu.make_async_remote_copy(
            src_ref=block, dst_ref=block,
            send_sem=g_send.at[k], recv_sem=g_recv.at[k],
            device_id={"tok": me + 1 - 2 * col},
        )

    def run_early(k):
        y_copies[k].wait_recv()
        mine = own[k] + yrecv[k].astype(jnp.float32)
        copy = chain_copy(early, k)

        @pl.when(rank > 0)
        def _():
            copy.wait_recv()

        total = mine + zin[early, k].astype(jnp.float32)
        zout[early, k] = total.astype(jnp.bfloat16)
        own[k] = mine
        prefix[k] = total
        copy.start()

    def run_late(k):
        copy = chain_copy(late, k)
        copy.wait_recv()
        incoming = zin[late, k].astype(jnp.float32)
        total = prefix[k] + incoming
        i, j, rows = piece(k, col)
        low = total.astype(jnp.bfloat16)

        @pl.when(rank > 0)
        def _():
            zout[late, k] = (own[k] + incoming).astype(jnp.bfloat16)
            copy.start()

        mlow[rows, strip(j)] = low
        block_copy(k).start()
        weight = jnp.where(i == j, 1.0, 2.0)
        sqacc[...] += weight * jnp.sum(total * total, axis=0, keepdims=True)

        @pl.when(i != j)
        def _():
            mlow[strip(j), rows] = total.T.astype(jnp.bfloat16)

    def run_chain(lag):
        for t in range(count + lag):
            if t < count:
                run_early(t)
            if t >= lag:
                run_late(t - lag)

    @pl.when(rank == 0)
    def _():
        run_chain(count)

    @pl.when(rank > 0)
    def _():
        run_chain(min(LAG, count))

    squared = jnp.sum(sqacc[...], axis=1, keepdims=True)
    losses[me] = jnp.broadcast_to(squared, losses.shape[1:])
    l_copies = gather_copies(losses, l_send, l_recv, "tok", me, n)
    for copy in l_copies:
        copy.start()

    for k in range(count):
        block_copy(k).wait_recv()
        i, j, rows = piece(k, 1 - col)

        @pl.when(i != j)
        def _():
            block = mlow[rows, strip(j)].astype(jnp.float32)
            mlow[strip(j), rows] = block.T.astype(jnp.bfloat16)

    @pl.loop(0, nb)
    def _(b):
        rows = strip(b)
        p = 4.0 * jnp.dot(mlow[rows, :], unit_low[...], preferred_element_type=jnp.float32)
        pull[rows, :] = p
        unit = sbuf[rows, :].astype(jnp.float32) * spread(inv[rows, :], feats)
        part[rows, :] = lane_tiles_sum(unit * p)

    pack_rows(along)
    a_copies = gather_copies(along, a_send, a_recv, "tok", me, n)
    for copy in a_copies:
        copy.start()

    for copy in l_copies:
        copy.wait_recv()
    img_losses[img] = summed(losses, n)
    i_copies = gather_copies(img_losses, i_send, i_recv, "img", img, m)
    for copy in i_copies:
        copy.start()

    for copy in a_copies:
        copy.wait_recv()
    unpack_rows(summed(along, n), tinv)

    @pl.loop(0, tiles)
    def _(b):
        scale = spread(inv[slab(b), :], feats)
        unit = sbuf[slab(b), :].astype(jnp.float32) * scale
        grad = scale * pull[slab(b), :] - scale * unit * spread(tinv[slab(b), :], feats)
        out_ref[0, slab(b), :] = grad.astype(out_ref.dtype)

    for copy in i_copies:
        copy.wait_recv()
    loss_ref[...] = summed(img_losses, m) / (chain * tokens)

    for copy in s_copies + t_copies + l_copies + a_copies + i_copies + y_copies:
        copy.wait_send()
    for k in range(count):
        block_copy(k).wait_send()
        chain_copy(early, k).wait_send()

        @pl.when(rank > 0)
        def _():
            chain_copy(late, k).wait_send()


def tap_matrix(width, rows_per):
    half = width // 2
    taps = np.zeros((half, width), np.float32)
    for b in range(half):
        for q in range(4):
            taps[b, min(max(2 * b - 1 + q, 0), width - 1)] += cubic_taps[q]
    return jnp.asarray(np.kron(np.eye(rows_per, dtype=np.float32), taps), jnp.bfloat16)


def per_device(n, m, student, teacher):
    _, tokens, feats = student.shape
    _, height, width, _ = teacher.shape
    rows_per = max(1, 256 // width)
    groups = height // rows_per
    nb = tokens // BLOCK
    half = nb * (nb + 1) // 4
    count = half * SPLIT
    depth = BLOCK // SPLIT
    tiles = tokens // LANES
    f32, bf16 = jnp.float32, jnp.bfloat16
    vmem, dma = pltpu.VMEM, pltpu.SemaphoreType.DMA
    gradient, loss = pl.pallas_call(
        functools.partial(kernel, (n, m)),
        name="anchor",
        out_shape=(
            jax.ShapeDtypeStruct(student.shape, bf16),
            jax.ShapeDtypeStruct((8, LANES), f32),
        ),
        in_specs=[
            pl.BlockSpec(memory_space=pl.ANY),
            pl.BlockSpec(memory_space=pl.ANY),
            pl.BlockSpec(memory_space=pltpu.VMEM),
        ],
        out_specs=(
            pl.BlockSpec(memory_space=pltpu.VMEM),
            pl.BlockSpec(memory_space=pltpu.VMEM),
        ),
        scratch_shapes=[
            vmem((tokens, feats), bf16),
            vmem((height, width, feats), bf16),
            vmem((height + 2, width // 2, feats), f32),
            vmem((tokens, feats), f32),
            vmem((tokens, feats), bf16),
            vmem((tokens, feats), bf16),
            vmem((tokens, LANES), f32),
            vmem((tokens, LANES), f32),
            vmem((tokens, LANES), f32),
            vmem((n, tiles, LANES), f32),
            vmem((n, tiles, LANES), f32),
            vmem((n, tiles, LANES), f32),
            vmem((n, 8, LANES), f32),
            vmem((m, 8, LANES), f32),
            vmem((count, depth, BLOCK), f32),
            vmem((count, depth, BLOCK), f32),
            vmem((half, BLOCK, BLOCK), f32),
            vmem((count, depth, BLOCK), bf16),
            vmem((count, depth, BLOCK), bf16),
            vmem((2, count, depth, BLOCK), bf16),
            vmem((2, count, depth, BLOCK), bf16),
            vmem((tokens, tokens), bf16),
            vmem((tokens, feats), f32),
            vmem((1, BLOCK), f32),
            dma((groups + 1,)),
            dma((n - 1,)), dma((n - 1,)), dma((n - 1,)), dma((n - 1,)),
            dma((n - 1,)), dma((n - 1,)), dma((n - 1,)), dma((n - 1,)),
            dma((m - 1,)), dma((m - 1,)),
            dma((count,)), dma((count,)),
            dma((2, count)), dma((2, count)),
            dma((count,)), dma((count,)),
        ],
        compiler_params=pltpu.CompilerParams(
            collective_id=0, has_side_effects=True, vmem_limit_bytes=56 * 1024 * 1024
        ),
    )(student, teacher, tap_matrix(width, rows_per))
    return gradient, loss[0, 0]


def solution(mesh):
    return jax.shard_map(
        functools.partial(per_device, mesh.shape["tok"], mesh.shape["img"]),
        mesh=mesh,
        in_specs=(P("img", None, "tok"), P("img", None, None, "tok")),
        out_specs=(P("img", None, "tok"), P()),
        check_vma=False,
    )
```

```python
import functools

import jax
import jax.numpy as jnp
import numpy as np
from jax import lax
from jax.experimental import pallas as pl
from jax.experimental.pallas import tpu as pltpu
from jax.sharding import PartitionSpec as P

cubic_taps = (-0.09375, 0.59375, 0.59375, -0.09375)
epsilon = 1e-06
LANES = 128
BLOCK = 256
SPLIT = 2
LAG = 2


def lane_tiles_sum(x):
    total = x[:, :LANES]
    for start in range(LANES, x.shape[1], LANES):
        total = total + x[:, start : start + LANES]
    return total


def spread(column, width):
    return jnp.concatenate([column] * (width // LANES), axis=1)


def kernel(
    sizes, student_hbm, teacher_hbm, taps_ref, out_ref, loss_ref,
    sbuf, tbuf, hbuf, shrunk, unit_low, teach_low, part, inv, tinv,
    snorm, tnorm, along, losses, img_losses,
    own, prefix, theirs, ysend, yrecv, zin, zout, mlow, pull, sqacc,
    load_sem, s_send, s_recv, t_send, t_recv, a_send, a_recv, l_send, l_recv,
    i_send, i_recv, y_send, y_recv, z_send, z_recv, g_send, g_recv,
):
    n, m = sizes
    tokens, feats = unit_low.shape
    height, width = tbuf.shape[0], tbuf.shape[1]
    group = load_sem.shape[0] - 1
    rows_per = height // group
    half_w = width // 2
    nb = tokens // BLOCK
    tiles = tokens // LANES
    me = lax.axis_index("tok")
    img = lax.axis_index("img")
    col = lax.rem(me, 2)
    row = me // 2
    chain = n // 2
    square = [(i, i) for i in range(nb)]
    upper = [(i, j) for i in range(nb) for j in range(i + 1, nb)]
    diag, off = len(square) // 2, len(upper) // 2
    pairs = square[:diag] + upper[:off] + square[diag:] + upper[off:]
    half = diag + off
    count = half * SPLIT
    depth = BLOCK // SPLIT
    early = jnp.where(row < (chain + 1) // 2, 0, 1)
    late = 1 - early
    rank = jnp.minimum(row, chain - 1 - row)

    def load(g):
        rows = pl.ds(g * rows_per, rows_per)
        return pltpu.make_async_copy(
            teacher_hbm.at[0, rows], tbuf.at[rows], load_sem.at[g]
        )

    student_load = pltpu.make_async_copy(student_hbm.at[0], sbuf, load_sem.at[group])
    student_load.start()

    @pl.loop(0, group)
    def _(g):
        load(g).start()

    barrier = pltpu.get_barrier_semaphore()
    for p in range(1, n):
        pl.semaphore_signal(barrier, 1, device_id={"tok": lax.rem(me + p, n)})
    for p in range(1, m):
        pl.semaphore_signal(barrier, 1, device_id={"img": lax.rem(img + p, m)})

    def gather_copies(buf, send, recv, axis, here, size):
        return [
            pltpu.make_async_remote_copy(
                src_ref=buf.at[here],
                dst_ref=buf.at[here],
                send_sem=send.at[p - 1],
                recv_sem=recv.at[p - 1],
                device_id={axis: lax.rem(here + p, size)},
            )
            for p in range(1, size)
        ]

    def pack_rows(buf):
        @pl.loop(0, tiles)
        def _(b):
            block = part[pl.ds(pl.multiple_of(b * LANES, LANES), LANES), :]
            buf[me, pl.ds(b, 1), :] = jnp.sum(block.T, axis=0, keepdims=True)

    def summed(buf, size):
        total = buf[0]
        for k in range(1, size):
            total = total + buf[k]
        return total

    def unpack_rows(values, dst):
        for b in range(tiles):
            dst[b * LANES : (b + 1) * LANES, :] = jnp.broadcast_to(
                values[b : b + 1, :], (LANES, LANES)
            ).T

    def slab(b):
        return pl.ds(pl.multiple_of(b * LANES, LANES), LANES)

    @pl.when(rank == 0)
    def _():
        zin[early] = jnp.zeros(zin.shape[1:], zin.dtype)

    sqacc[...] = jnp.zeros_like(sqacc)
    student_load.wait()

    @pl.loop(0, tiles)
    def _(b):
        x = sbuf[slab(b), :].astype(jnp.float32)
        part[slab(b), :] = lane_tiles_sum(x * x)

    pack_rows(snorm)
    @pl.loop(0, group)
    def _(g):
        load(g).wait()
        x = tbuf[pl.ds(g * rows_per, rows_per)].reshape(rows_per * width, feats)
        y = jnp.dot(taps_ref[...], x, preferred_element_type=jnp.float32)
        hbuf[pl.ds(g * rows_per + 1, rows_per)] = y.reshape(rows_per, half_w, feats)

    pl.semaphore_wait(barrier, n - 1 + m - 1)
    s_copies = gather_copies(snorm, s_send, s_recv, "tok", me, n)
    for copy in s_copies:
        copy.start()

    hbuf[0] = hbuf[1]
    hbuf[height + 1] = hbuf[height]

    @pl.loop(0, height // 2)
    def _(a):
        v = cubic_taps[0] * hbuf[2 * a]
        for k in range(1, 4):
            v = v + cubic_taps[k] * hbuf[2 * a + k]
        rows = pl.ds(pl.multiple_of(a * half_w, half_w), half_w)
        shrunk[rows, :] = v
        part[rows, :] = lane_tiles_sum(v * v)

    pack_rows(tnorm)
    t_copies = gather_copies(tnorm, t_send, t_recv, "tok", me, n)
    for copy in t_copies:
        copy.start()

    for copy in s_copies:
        copy.wait_recv()
    unpack_rows(lax.rsqrt(summed(snorm, n) + epsilon), inv)

    @pl.loop(0, tiles)
    def _(b):
        x = sbuf[slab(b), :].astype(jnp.float32) * spread(inv[slab(b), :], feats)
        unit_low[slab(b), :] = x.astype(jnp.bfloat16)

    def pick(k, c):
        first, second = pairs[k], pairs[half + k]
        i = first[0] + c * (second[0] - first[0])
        j = first[1] + c * (second[1] - first[1])
        return i, j

    def strip(i):
        return pl.ds(pl.multiple_of(i * BLOCK, BLOCK), BLOCK)

    def gram(low, i, j):
        return lax.dot_general(
            low[strip(i), :], low[strip(j), :], (((1,), (1,)), ((), ())),
            preferred_element_type=jnp.float32,
        )

    for k in range(half):
        theirs[k] = gram(unit_low, *pick(k, 1 - col))
    for k in range(half):
        pieces = gram(unit_low, *pick(k, col))
        own[k * SPLIT : (k + 1) * SPLIT] = pieces.reshape(SPLIT, depth, BLOCK)

    for copy in t_copies:
        copy.wait_recv()
    unpack_rows(lax.rsqrt(summed(tnorm, n) + epsilon), tinv)

    @pl.loop(0, tiles)
    def _(b):
        x = shrunk[slab(b), :] * spread(tinv[slab(b), :], feats)
        teach_low[slab(b), :] = x.astype(jnp.bfloat16)

    def skip(k):
        return (k % SPLIT) * depth if k < diag * SPLIT else 0

    y_copies = []
    for k in range(half):
        d = theirs[k] - gram(teach_low, *pick(k, 1 - col))
        pieces = d.astype(jnp.bfloat16).reshape(SPLIT, depth, BLOCK)
        ysend[k * SPLIT : (k + 1) * SPLIT] = pieces
        for t in range(k * SPLIT, (k + 1) * SPLIT):
            copy = pltpu.make_async_remote_copy(
                src_ref=ysend.at[t, :, skip(t) :], dst_ref=yrecv.at[t, :, skip(t) :],
                send_sem=y_send.at[t], recv_sem=y_recv.at[t],
                device_id={"tok": me + 1 - 2 * col},
            )
            copy.start()
            y_copies.append(copy)
    for k in range(half):
        d = gram(teach_low, *pick(k, col)).reshape(SPLIT, depth, BLOCK)
        own[k * SPLIT : (k + 1) * SPLIT] = own[k * SPLIT : (k + 1) * SPLIT] - d

    def chain_copy(direction, k):
        step = 2 - 4 * direction
        return pltpu.make_async_remote_copy(
            src_ref=zout.at[direction, k, :, skip(k) :],
            dst_ref=zin.at[direction, k, :, skip(k) :],
            send_sem=z_send.at[direction, k], recv_sem=z_recv.at[direction, k],
            device_id={"tok": lax.rem(me + step + n, n)},
        )

    def piece(k, c):
        i, j = pick(k // SPLIT, c)
        start = i * BLOCK + (k % SPLIT) * depth
        columns = pl.ds(pl.multiple_of(j * BLOCK + skip(k), depth), BLOCK - skip(k))
        return i, j, pl.ds(pl.multiple_of(start, depth), depth), columns

    def mirror(k, c, block):
        _, j, rows, _ = piece(k, c)
        first = 0
        if k < diag * SPLIT:
            first = skip(k) + depth
            block = block[:, depth:]
        if first < BLOCK:
            start = pl.multiple_of(j * BLOCK + first, depth)
            mlow[pl.ds(start, BLOCK - first), rows] = block.T.astype(jnp.bfloat16)

    def block_copy(k):
        _, _, rows, columns = piece(k, col)
        block = mlow.at[rows, columns]
        return pltpu.make_async_remote_copy(
            src_ref=block, dst_ref=block,
            send_sem=g_send.at[k], recv_sem=g_recv.at[k],
            device_id={"tok": me + 1 - 2 * col},
        )

    def run_early(k):
        y_copies[k].wait_recv()
        cut = skip(k)
        mine = own[k, :, cut:] + yrecv[k, :, cut:].astype(jnp.float32)
        copy = chain_copy(early, k)

        @pl.when(rank > 0)
        def _():
            copy.wait_recv()

        total = mine + zin[early, k, :, cut:].astype(jnp.float32)
        zout[early, k, :, cut:] = total.astype(jnp.bfloat16)
        own[k, :, cut:] = mine
        prefix[k, :, cut:] = total
        copy.start()

    def run_late(k):
        copy = chain_copy(late, k)
        copy.wait_recv()
        cut = skip(k)
        incoming = zin[late, k, :, cut:].astype(jnp.float32)
        total = prefix[k, :, cut:] + incoming
        _, _, rows, columns = piece(k, col)
        low = total.astype(jnp.bfloat16)

        @pl.when(rank > 0)
        def _():
            zout[late, k, :, cut:] = (own[k, :, cut:] + incoming).astype(jnp.bfloat16)
            copy.start()

        mlow[rows, columns] = low
        block_copy(k).start()
        sums = jnp.sum(total * total, axis=0, keepdims=True)
        if k < diag * SPLIT:
            sqacc[:, :depth] += sums[:, :depth]
            if cut + depth < BLOCK:
                sqacc[:, cut + depth :] += 2.0 * sums[:, depth:]
        else:
            sqacc[...] += 2.0 * sums
        mirror(k, col, total)

    def run_chain(lag):
        for t in range(count + lag):
            if t < count:
                run_early(t)
            if t >= lag:
                run_late(t - lag)

    @pl.when(rank == 0)
    def _():
        run_chain(count)

    @pl.when(rank > 0)
    def _():
        run_chain(min(LAG, count))

    squared = jnp.sum(sqacc[...], axis=1, keepdims=True)
    losses[me] = jnp.broadcast_to(squared, losses.shape[1:])
    l_copies = gather_copies(losses, l_send, l_recv, "tok", me, n)
    for copy in l_copies:
        copy.start()

    for k in range(count):
        block_copy(k).wait_recv()
        _, _, rows, columns = piece(k, 1 - col)
        mirror(k, 1 - col, mlow[rows, columns].astype(jnp.float32))

    @pl.loop(0, nb)
    def _(b):
        rows = strip(b)
        p = 4.0 * jnp.dot(mlow[rows, :], unit_low[...], preferred_element_type=jnp.float32)
        pull[rows, :] = p
        unit = sbuf[rows, :].astype(jnp.float32) * spread(inv[rows, :], feats)
        part[rows, :] = lane_tiles_sum(unit * p)

    pack_rows(along)
    a_copies = gather_copies(along, a_send, a_recv, "tok", me, n)
    for copy in a_copies:
        copy.start()

    for copy in l_copies:
        copy.wait_recv()
    img_losses[img] = summed(losses, n)
    i_copies = gather_copies(img_losses, i_send, i_recv, "img", img, m)
    for copy in i_copies:
        copy.start()

    for copy in a_copies:
        copy.wait_recv()
    unpack_rows(summed(along, n), tinv)

    @pl.loop(0, tiles)
    def _(b):
        scale = spread(inv[slab(b), :], feats)
        unit = sbuf[slab(b), :].astype(jnp.float32) * scale
        grad = scale * pull[slab(b), :] - scale * unit * spread(tinv[slab(b), :], feats)
        out_ref[0, slab(b), :] = grad.astype(out_ref.dtype)

    for copy in i_copies:
        copy.wait_recv()
    loss_ref[...] = summed(img_losses, m) / (chain * tokens)

    for copy in s_copies + t_copies + l_copies + a_copies + i_copies + y_copies:
        copy.wait_send()
    for k in range(count):
        block_copy(k).wait_send()
        chain_copy(early, k).wait_send()

        @pl.when(rank > 0)
        def _():
            chain_copy(late, k).wait_send()


def tap_matrix(width, rows_per):
    half = width // 2
    taps = np.zeros((half, width), np.float32)
    for b in range(half):
        for q in range(4):
            taps[b, min(max(2 * b - 1 + q, 0), width - 1)] += cubic_taps[q]
    return jnp.asarray(np.kron(np.eye(rows_per, dtype=np.float32), taps), jnp.bfloat16)


def per_device(n, m, student, teacher):
    _, tokens, feats = student.shape
    _, height, width, _ = teacher.shape
    rows_per = max(1, 256 // width)
    groups = height // rows_per
    nb = tokens // BLOCK
    half = nb // 2 + nb * (nb - 1) // 4
    count = half * SPLIT
    depth = BLOCK // SPLIT
    tiles = tokens // LANES
    f32, bf16 = jnp.float32, jnp.bfloat16
    vmem, dma = pltpu.VMEM, pltpu.SemaphoreType.DMA
    gradient, loss = pl.pallas_call(
        functools.partial(kernel, (n, m)),
        name="anchor",
        out_shape=(
            jax.ShapeDtypeStruct(student.shape, bf16),
            jax.ShapeDtypeStruct((8, LANES), f32),
        ),
        in_specs=[
            pl.BlockSpec(memory_space=pl.ANY),
            pl.BlockSpec(memory_space=pl.ANY),
            pl.BlockSpec(memory_space=pltpu.VMEM),
        ],
        out_specs=(
            pl.BlockSpec(memory_space=pltpu.VMEM),
            pl.BlockSpec(memory_space=pltpu.VMEM),
        ),
        scratch_shapes=[
            vmem((tokens, feats), bf16),
            vmem((height, width, feats), bf16),
            vmem((height + 2, width // 2, feats), f32),
            vmem((tokens, feats), f32),
            vmem((tokens, feats), bf16),
            vmem((tokens, feats), bf16),
            vmem((tokens, LANES), f32),
            vmem((tokens, LANES), f32),
            vmem((tokens, LANES), f32),
            vmem((n, tiles, LANES), f32),
            vmem((n, tiles, LANES), f32),
            vmem((n, tiles, LANES), f32),
            vmem((n, 8, LANES), f32),
            vmem((m, 8, LANES), f32),
            vmem((count, depth, BLOCK), f32),
            vmem((count, depth, BLOCK), f32),
            vmem((half, BLOCK, BLOCK), f32),
            vmem((count, depth, BLOCK), bf16),
            vmem((count, depth, BLOCK), bf16),
            vmem((2, count, depth, BLOCK), bf16),
            vmem((2, count, depth, BLOCK), bf16),
            vmem((tokens, tokens), bf16),
            vmem((tokens, feats), f32),
            vmem((1, BLOCK), f32),
            dma((groups + 1,)),
            dma((n - 1,)), dma((n - 1,)), dma((n - 1,)), dma((n - 1,)),
            dma((n - 1,)), dma((n - 1,)), dma((n - 1,)), dma((n - 1,)),
            dma((m - 1,)), dma((m - 1,)),
            dma((count,)), dma((count,)),
            dma((2, count)), dma((2, count)),
            dma((count,)), dma((count,)),
        ],
        compiler_params=pltpu.CompilerParams(
            collective_id=0, has_side_effects=True, vmem_limit_bytes=56 * 1024 * 1024
        ),
    )(student, teacher, tap_matrix(width, rows_per))
    return gradient, loss[0, 0]


def solution(mesh):
    return jax.shard_map(
        functools.partial(per_device, mesh.shape["tok"], mesh.shape["img"]),
        mesh=mesh,
        in_specs=(P("img", None, "tok"), P("img", None, None, "tok")),
        out_specs=(P("img", None, "tok"), P()),
        check_vma=False,
    )
```

```python
import functools

import jax
import jax.numpy as jnp
import numpy as np
from jax import lax
from jax.experimental import pallas as pl
from jax.experimental.pallas import tpu as pltpu
from jax.sharding import PartitionSpec as P

cubic_taps = (-0.09375, 0.59375, 0.59375, -0.09375)
epsilon = 1e-06
LANES = 128
BLOCK = 256
SPLIT = 2
LAG = 2


def lane_tiles_sum(x):
    total = x[:, :LANES]
    for start in range(LANES, x.shape[1], LANES):
        total = total + x[:, start : start + LANES]
    return total


def spread(column, width):
    return jnp.concatenate([column] * (width // LANES), axis=1)


def kernel(
    sizes, student_hbm, teacher_hbm, taps_ref, out_ref, loss_ref,
    sbuf, tbuf, hbuf, shrunk, unit_low, teach_low, part, inv, tinv,
    snorm, tnorm, along, losses, img_losses,
    own, prefix, theirs, ysend, yrecv, zin, zout, mlow, pull, sqacc,
    load_sem, s_send, s_recv, t_send, t_recv, a_send, a_recv, l_send, l_recv,
    i_send, i_recv, y_send, y_recv, z_send, z_recv, g_send, g_recv,
):
    n, m = sizes
    tokens, feats = unit_low.shape
    height, width = tbuf.shape[0], tbuf.shape[1]
    group = load_sem.shape[0] - 1
    rows_per = height // group
    half_w = width // 2
    nb = tokens // BLOCK
    tiles = tokens // LANES
    me = lax.axis_index("tok")
    img = lax.axis_index("img")
    col = lax.rem(me, 2)
    row = me // 2
    chain = n // 2
    square = [(i, i) for i in range(nb)]
    upper = [(i, j) for i in range(nb) for j in range(i + 1, nb)]
    diag, off = len(square) // 2, len(upper) // 2
    pairs = upper[:off] + square[:diag] + upper[off:] + square[diag:]
    half = diag + off
    count = half * SPLIT
    depth = BLOCK // SPLIT
    early = jnp.where(row < (chain + 1) // 2, 0, 1)
    late = 1 - early
    rank = jnp.minimum(row, chain - 1 - row)

    def load(g):
        rows = pl.ds(g * rows_per, rows_per)
        return pltpu.make_async_copy(
            teacher_hbm.at[0, rows], tbuf.at[rows], load_sem.at[g]
        )

    student_load = pltpu.make_async_copy(student_hbm.at[0], sbuf, load_sem.at[group])
    student_load.start()

    @pl.loop(0, group)
    def _(g):
        load(g).start()

    barrier = pltpu.get_barrier_semaphore()
    for p in range(1, n):
        pl.semaphore_signal(barrier, 1, device_id={"tok": lax.rem(me + p, n)})
    for p in range(1, m):
        pl.semaphore_signal(barrier, 1, device_id={"img": lax.rem(img + p, m)})

    def gather_copies(buf, send, recv, axis, here, size):
        return [
            pltpu.make_async_remote_copy(
                src_ref=buf.at[here],
                dst_ref=buf.at[here],
                send_sem=send.at[p - 1],
                recv_sem=recv.at[p - 1],
                device_id={axis: lax.rem(here + p, size)},
            )
            for p in range(1, size)
        ]

    def pack_rows(buf):
        @pl.loop(0, tiles)
        def _(b):
            block = part[pl.ds(pl.multiple_of(b * LANES, LANES), LANES), :]
            buf[me, pl.ds(b, 1), :] = jnp.sum(block.T, axis=0, keepdims=True)

    def summed(buf, size):
        total = buf[0]
        for k in range(1, size):
            total = total + buf[k]
        return total

    def unpack_rows(values, dst):
        for b in range(tiles):
            dst[b * LANES : (b + 1) * LANES, :] = jnp.broadcast_to(
                values[b : b + 1, :], (LANES, LANES)
            ).T

    def slab(b):
        return pl.ds(pl.multiple_of(b * LANES, LANES), LANES)

    @pl.when(rank == 0)
    def _():
        zin[early] = jnp.zeros(zin.shape[1:], zin.dtype)

    sqacc[...] = jnp.zeros_like(sqacc)
    student_load.wait()

    @pl.loop(0, tiles)
    def _(b):
        x = sbuf[slab(b), :].astype(jnp.float32)
        part[slab(b), :] = lane_tiles_sum(x * x)

    pack_rows(snorm)
    @pl.loop(0, group)
    def _(g):
        load(g).wait()
        x = tbuf[pl.ds(g * rows_per, rows_per)].reshape(rows_per * width, feats)
        y = jnp.dot(taps_ref[...], x, preferred_element_type=jnp.float32)
        hbuf[pl.ds(g * rows_per + 1, rows_per)] = y.reshape(rows_per, half_w, feats)

    pl.semaphore_wait(barrier, n - 1 + m - 1)
    s_copies = gather_copies(snorm, s_send, s_recv, "tok", me, n)
    for copy in s_copies:
        copy.start()

    hbuf[0] = hbuf[1]
    hbuf[height + 1] = hbuf[height]

    @pl.loop(0, height // 2)
    def _(a):
        v = cubic_taps[0] * hbuf[2 * a]
        for k in range(1, 4):
            v = v + cubic_taps[k] * hbuf[2 * a + k]
        rows = pl.ds(pl.multiple_of(a * half_w, half_w), half_w)
        shrunk[rows, :] = v
        part[rows, :] = lane_tiles_sum(v * v)

    pack_rows(tnorm)
    t_copies = gather_copies(tnorm, t_send, t_recv, "tok", me, n)
    for copy in t_copies:
        copy.start()

    for copy in s_copies:
        copy.wait_recv()
    unpack_rows(lax.rsqrt(summed(snorm, n) + epsilon), inv)

    @pl.loop(0, tiles)
    def _(b):
        x = sbuf[slab(b), :].astype(jnp.float32) * spread(inv[slab(b), :], feats)
        unit_low[slab(b), :] = x.astype(jnp.bfloat16)

    def pick(k, c):
        first, second = pairs[k], pairs[half + k]
        i = first[0] + c * (second[0] - first[0])
        j = first[1] + c * (second[1] - first[1])
        return i, j

    def strip(i):
        return pl.ds(pl.multiple_of(i * BLOCK, BLOCK), BLOCK)

    def gram(low, i, j):
        return lax.dot_general(
            low[strip(i), :], low[strip(j), :], (((1,), (1,)), ((), ())),
            preferred_element_type=jnp.float32,
        )

    for k in range(half):
        theirs[k] = gram(unit_low, *pick(k, 1 - col))
    for k in range(half):
        pieces = gram(unit_low, *pick(k, col))
        own[k * SPLIT : (k + 1) * SPLIT] = pieces.reshape(SPLIT, depth, BLOCK)

    for copy in t_copies:
        copy.wait_recv()
    unpack_rows(lax.rsqrt(summed(tnorm, n) + epsilon), tinv)

    @pl.loop(0, tiles)
    def _(b):
        x = shrunk[slab(b), :] * spread(tinv[slab(b), :], feats)
        teach_low[slab(b), :] = x.astype(jnp.bfloat16)

    def skip(k):
        return (k % SPLIT) * depth if k >= off * SPLIT else 0

    y_copies = []
    for k in range(half):
        d = theirs[k] - gram(teach_low, *pick(k, 1 - col))
        pieces = d.astype(jnp.bfloat16).reshape(SPLIT, depth, BLOCK)
        ysend[k * SPLIT : (k + 1) * SPLIT] = pieces
        for t in range(k * SPLIT, (k + 1) * SPLIT):
            copy = pltpu.make_async_remote_copy(
                src_ref=ysend.at[t, :, skip(t) :], dst_ref=yrecv.at[t, :, skip(t) :],
                send_sem=y_send.at[t], recv_sem=y_recv.at[t],
                device_id={"tok": me + 1 - 2 * col},
            )
            copy.start()
            y_copies.append(copy)
    for k in range(half):
        d = gram(teach_low, *pick(k, col)).reshape(SPLIT, depth, BLOCK)
        own[k * SPLIT : (k + 1) * SPLIT] = own[k * SPLIT : (k + 1) * SPLIT] - d

    def chain_copy(direction, k):
        step = 2 - 4 * direction
        return pltpu.make_async_remote_copy(
            src_ref=zout.at[direction, k, :, skip(k) :],
            dst_ref=zin.at[direction, k, :, skip(k) :],
            send_sem=z_send.at[direction, k], recv_sem=z_recv.at[direction, k],
            device_id={"tok": lax.rem(me + step + n, n)},
        )

    def piece(k, c):
        i, j = pick(k // SPLIT, c)
        start = i * BLOCK + (k % SPLIT) * depth
        columns = pl.ds(pl.multiple_of(j * BLOCK + skip(k), depth), BLOCK - skip(k))
        return i, j, pl.ds(pl.multiple_of(start, depth), depth), columns

    def mirror(k, c, block):
        _, j, rows, _ = piece(k, c)
        first = 0
        if k >= off * SPLIT:
            first = skip(k) + depth
            block = block[:, depth:]
        if first < BLOCK:
            start = pl.multiple_of(j * BLOCK + first, depth)
            mlow[pl.ds(start, BLOCK - first), rows] = block.T.astype(jnp.bfloat16)

    def block_copy(k):
        _, _, rows, columns = piece(k, col)
        block = mlow.at[rows, columns]
        return pltpu.make_async_remote_copy(
            src_ref=block, dst_ref=block,
            send_sem=g_send.at[k], recv_sem=g_recv.at[k],
            device_id={"tok": me + 1 - 2 * col},
        )

    def run_early(k):
        y_copies[k].wait_recv()
        cut = skip(k)
        mine = own[k, :, cut:] + yrecv[k, :, cut:].astype(jnp.float32)
        copy = chain_copy(early, k)

        @pl.when(rank > 0)
        def _():
            copy.wait_recv()

        total = mine + zin[early, k, :, cut:].astype(jnp.float32)
        zout[early, k, :, cut:] = total.astype(jnp.bfloat16)
        own[k, :, cut:] = mine
        prefix[k, :, cut:] = total
        copy.start()

    def run_late(k):
        copy = chain_copy(late, k)
        copy.wait_recv()
        cut = skip(k)
        incoming = zin[late, k, :, cut:].astype(jnp.float32)
        total = prefix[k, :, cut:] + incoming
        _, _, rows, columns = piece(k, col)
        low = total.astype(jnp.bfloat16)

        @pl.when(rank > 0)
        def _():
            zout[late, k, :, cut:] = (own[k, :, cut:] + incoming).astype(jnp.bfloat16)
            copy.start()

        mlow[rows, columns] = low
        block_copy(k).start()
        sums = jnp.sum(total * total, axis=0, keepdims=True)
        if k >= off * SPLIT:
            sqacc[:, :depth] += sums[:, :depth]
            if cut + depth < BLOCK:
                sqacc[:, cut + depth :] += 2.0 * sums[:, depth:]
        else:
            sqacc[...] += 2.0 * sums
        mirror(k, col, total)

    def run_chain(lag):
        for t in range(count + lag):
            if t < count:
                run_early(t)
            if t >= lag:
                run_late(t - lag)

    @pl.when(rank == 0)
    def _():
        run_chain(count)

    @pl.when(rank > 0)
    def _():
        run_chain(min(LAG, count))

    squared = jnp.sum(sqacc[...], axis=1, keepdims=True)
    losses[me] = jnp.broadcast_to(squared, losses.shape[1:])
    l_copies = gather_copies(losses, l_send, l_recv, "tok", me, n)
    for copy in l_copies:
        copy.start()

    for k in range(count):
        block_copy(k).wait_recv()
        _, _, rows, columns = piece(k, 1 - col)
        mirror(k, 1 - col, mlow[rows, columns].astype(jnp.float32))

    @pl.loop(0, nb)
    def _(b):
        rows = strip(b)
        p = 4.0 * jnp.dot(mlow[rows, :], unit_low[...], preferred_element_type=jnp.float32)
        pull[rows, :] = p
        unit = sbuf[rows, :].astype(jnp.float32) * spread(inv[rows, :], feats)
        part[rows, :] = lane_tiles_sum(unit * p)

    pack_rows(along)
    a_copies = gather_copies(along, a_send, a_recv, "tok", me, n)
    for copy in a_copies:
        copy.start()

    for copy in l_copies:
        copy.wait_recv()
    img_losses[img] = summed(losses, n)
    i_copies = gather_copies(img_losses, i_send, i_recv, "img", img, m)
    for copy in i_copies:
        copy.start()

    for copy in a_copies:
        copy.wait_recv()
    unpack_rows(summed(along, n), tinv)

    @pl.loop(0, tiles)
    def _(b):
        scale = spread(inv[slab(b), :], feats)
        unit = sbuf[slab(b), :].astype(jnp.float32) * scale
        grad = scale * pull[slab(b), :] - scale * unit * spread(tinv[slab(b), :], feats)
        out_ref[0, slab(b), :] = grad.astype(out_ref.dtype)

    for copy in i_copies:
        copy.wait_recv()
    loss_ref[...] = summed(img_losses, m) / (chain * tokens)

    for copy in s_copies + t_copies + l_copies + a_copies + i_copies + y_copies:
        copy.wait_send()
    for k in range(count):
        block_copy(k).wait_send()
        chain_copy(early, k).wait_send()

        @pl.when(rank > 0)
        def _():
            chain_copy(late, k).wait_send()


def tap_matrix(width, rows_per):
    half = width // 2
    taps = np.zeros((half, width), np.float32)
    for b in range(half):
        for q in range(4):
            taps[b, min(max(2 * b - 1 + q, 0), width - 1)] += cubic_taps[q]
    return jnp.asarray(np.kron(np.eye(rows_per, dtype=np.float32), taps), jnp.bfloat16)


def per_device(n, m, student, teacher):
    _, tokens, feats = student.shape
    _, height, width, _ = teacher.shape
    rows_per = max(1, 256 // width)
    groups = height // rows_per
    nb = tokens // BLOCK
    half = nb // 2 + nb * (nb - 1) // 4
    count = half * SPLIT
    depth = BLOCK // SPLIT
    tiles = tokens // LANES
    f32, bf16 = jnp.float32, jnp.bfloat16
    vmem, dma = pltpu.VMEM, pltpu.SemaphoreType.DMA
    gradient, loss = pl.pallas_call(
        functools.partial(kernel, (n, m)),
        name="anchor",
        out_shape=(
            jax.ShapeDtypeStruct(student.shape, bf16),
            jax.ShapeDtypeStruct((8, LANES), f32),
        ),
        in_specs=[
            pl.BlockSpec(memory_space=pl.ANY),
            pl.BlockSpec(memory_space=pl.ANY),
            pl.BlockSpec(memory_space=pltpu.VMEM),
        ],
        out_specs=(
            pl.BlockSpec(memory_space=pltpu.VMEM),
            pl.BlockSpec(memory_space=pltpu.VMEM),
        ),
        scratch_shapes=[
            vmem((tokens, feats), bf16),
            vmem((height, width, feats), bf16),
            vmem((height + 2, width // 2, feats), f32),
            vmem((tokens, feats), f32),
            vmem((tokens, feats), bf16),
            vmem((tokens, feats), bf16),
            vmem((tokens, LANES), f32),
            vmem((tokens, LANES), f32),
            vmem((tokens, LANES), f32),
            vmem((n, tiles, LANES), f32),
            vmem((n, tiles, LANES), f32),
            vmem((n, tiles, LANES), f32),
            vmem((n, 8, LANES), f32),
            vmem((m, 8, LANES), f32),
            vmem((count, depth, BLOCK), f32),
            vmem((count, depth, BLOCK), f32),
            vmem((half, BLOCK, BLOCK), f32),
            vmem((count, depth, BLOCK), bf16),
            vmem((count, depth, BLOCK), bf16),
            vmem((2, count, depth, BLOCK), bf16),
            vmem((2, count, depth, BLOCK), bf16),
            vmem((tokens, tokens), bf16),
            vmem((tokens, feats), f32),
            vmem((1, BLOCK), f32),
            dma((groups + 1,)),
            dma((n - 1,)), dma((n - 1,)), dma((n - 1,)), dma((n - 1,)),
            dma((n - 1,)), dma((n - 1,)), dma((n - 1,)), dma((n - 1,)),
            dma((m - 1,)), dma((m - 1,)),
            dma((count,)), dma((count,)),
            dma((2, count)), dma((2, count)),
            dma((count,)), dma((count,)),
        ],
        compiler_params=pltpu.CompilerParams(
            collective_id=0, has_side_effects=True, vmem_limit_bytes=56 * 1024 * 1024
        ),
    )(student, teacher, tap_matrix(width, rows_per))
    return gradient, loss[0, 0]


def solution(mesh):
    return jax.shard_map(
        functools.partial(per_device, mesh.shape["tok"], mesh.shape["img"]),
        mesh=mesh,
        in_specs=(P("img", None, "tok"), P("img", None, None, "tok")),
        out_specs=(P("img", None, "tok"), P()),
        check_vma=False,
    )
```
